1024 devices in a mesh: row: 32 (over z, core), col: 8 (over y), rep: 4 (over x).
Axes of the slice: x: 4, y: 8, z: 16, core: 2. Of those that a mesh axis runs over, the one named last changes fastest.
Arguments:
- momentum: float32 [4, 8192, 8192], P('rep', 'row', 'col'), may hold values from -6 to 6
- gradient: bfloat16 [4, 8192, 8192], P('rep', 'row', 'col'), may hold values from -6 to 6
- weight: float32 [8192, 8192], P('row', 'col'), may hold values from -0.0625 to 0.0625
- right_basis: float32 [8192, 256], P('col'), may hold values from -6 to 6
Outputs:
- new_momentum: float32 [4, 8192, 8192], P('rep', 'row', 'col')
- new_weight: float32 [8192, 8192], P('row', 'col')
- new_basis: float32 [8192, 256], P('col')
The draws below stay inside these ranges and needn't reach their ends.
All inputs are finite; a program needn't handle non-finite values.
Results may differ from the reference program's by a relative error of at most 0.0012.
Values sent between devices are 32-bit elements; how exact they have to be, the bound alone decides.
A program may use at most 32 MiB of HBM per device.

```python
import jax
import jax.numpy as jnp
from jax import lax

D = 8192
RANK = 256
ITERS = 2
REPS = 4


def block_levels(key, extent, split, low, largest):
    loudness = 1.0
    for position, parts in split:
        draws = jax.random.uniform(jax.random.fold_in(jax.random.fold_in(key, 6), position), (parts,), jnp.float32, low / len(split), largest / len(split))
        loudness = loudness * jnp.repeat(jnp.exp(draws), extent[position] // parts).reshape((-1,) + (1,) * (len(extent) - 1 - position))
    return loudness


def scatter_about(stream_key, shape, scale, bound, shards=(), held_as=jnp.bfloat16):
    drawn = scale * jax.random.normal(stream_key, shape, jnp.float32)
    if shards:
        drawn = drawn * block_levels(stream_key, shape, shards, -0.22, 0.18)
    return jnp.clip(drawn, -bound, bound).astype(held_as)


def setup_inputs(seed: int = 0) -> dict:
    seeds = jax.random.split(jax.random.key(seed), 5)
    return {
        "momentum": scatter_about(seeds[0], (REPS, D, D), 1.0, 6.0, ((0, 4), (1, 32), (2, 8)), jnp.float32),
        "gradient": scatter_about(seeds[1], (REPS, D, D), 1.0, 6.0, ((0, 4), (1, 32), (2, 8))),
        "weight": scatter_about(seeds[2], (D, D), D ** -0.5, 0.0625, ((0, 32), (1, 8)), jnp.float32),
        "right_basis": scatter_about(seeds[3], (D, RANK), 1.0, 6.0, ((0, 8),), jnp.float32),
    }


beta_mom = 0.95
learn_rate = 0.05

def reference(momentum, gradient, weight, right_basis):
    highest = lax.Precision.HIGHEST
    buffer = momentum + gradient.astype(jnp.float32)
    mean_buffer = lax.optimization_barrier(jnp.mean(buffer, axis=0))
    basis_now = right_basis
    ortho = None
    factor = None
    for sweep in range(ITERS):
        left = jnp.dot(mean_buffer.astype(jnp.float32), basis_now.astype(jnp.float32), precision=highest, preferred_element_type=jnp.float32)
        gram_full = jnp.dot(left.T.astype(jnp.float32), left.astype(jnp.float32), precision=highest, preferred_element_type=jnp.float32)
        low_factor = jnp.linalg.cholesky(gram_full)
        ortho = jax.scipy.linalg.solve_triangular(low_factor, left.T, lower=True).T
        factor = jnp.dot(mean_buffer.T.astype(jnp.float32), ortho.astype(jnp.float32), precision=highest, preferred_element_type=jnp.float32)
        rms_cols = jnp.sqrt(lax.optimization_barrier(jnp.mean(factor * factor, axis=0)) + 1e-06)
        basis_now = factor / rms_cols
    feedback = jnp.dot(ortho.astype(jnp.float32), factor.T.astype(jnp.float32), precision=highest, preferred_element_type=jnp.float32)
    new_momentum = buffer - (1.0 - beta_mom) * feedback[None]
    update = jnp.dot(ortho.astype(jnp.float32), basis_now.T.astype(jnp.float32), precision=highest, preferred_element_type=jnp.float32)
    new_weight = weight - learn_rate * jnp.sqrt(jnp.float32(D) / jnp.float32(RANK)) * update
    return (new_momentum, new_weight, basis_now)
```

```python
import functools

import jax
import jax.numpy as jnp
from jax import lax
from jax.experimental import pallas as pl
from jax.experimental.pallas import tpu as pltpu
from jax.sharding import PartitionSpec as P

beta_mom = 0.95
learn_rate = 0.05
CORES = 2
TILE = 8
LANES = 128
HIGHEST = lax.Precision.HIGHEST
MESH = pl.DeviceIdType.MESH


def dot(a, b, over):
    return lax.dot_general(
        a, b, (over, ((), ())), precision=HIGHEST, preferred_element_type=jnp.float32
    )


def rows_by_rows(a, b):
    return dot(a, b, ((1,), (0,)))


def by_transposed(a, b):
    return dot(a, b, ((1,), (1,)))


def transposed_by(a, b):
    return dot(a, b, ((0,), (0,)))


class Cholesky:
    def __init__(self, work):
        self.work = work
        self.n = work.shape[0]
        self.panel = min(128, self.n)

    def load(self, gram):
        n = self.n
        self.work[:, :n] = gram
        eye = lax.broadcasted_iota(jnp.int32, (n, n), 0) == lax.broadcasted_iota(
            jnp.int32, (n, n), 1
        )
        self.work[:, n:] = jnp.where(eye, 1.0, 0.0)

    def blocks(self, first, last):
        work, n, size = self.work, self.n, self.panel
        base = (first * TILE // size) * size
        sub = lax.broadcasted_iota(jnp.int32, (TILE, LANES), 0)
        in_panel = lax.broadcasted_iota(jnp.int32, (size, 1), 0)

        def block(t, carry):
            start = pl.multiple_of(t * TILE, TILE)
            rows = work[pl.ds(start, TILE), :]
            small = pltpu.roll(rows[:, :n], lax.rem(n - start, n), 1)[:, :LANES]
            whole = (TILE, LANES)
            columns = [jnp.broadcast_to(small[:, i : i + 1], whole) for i in range(TILE)]
            a = {
                (r, i): jnp.broadcast_to(columns[i][r : r + 1, :], whole)
                for i in range(TILE)
                for r in range(i, TILE)
            }
            low, inv = {}, {}
            for i in range(TILE):
                root = lax.rsqrt(a[i, i])
                inv[i, i] = root
                for r in range(i + 1, TILE):
                    low[r, i] = a[r, i] * root
                for r in range(i + 1, TILE):
                    for c in range(i + 1, r + 1):
                        a[r, c] = a[r, c] - low[r, i] * low[c, i]
                for c in range(i):
                    acc = low[i, c] * inv[c, c]
                    for k in range(c + 1, i):
                        acc = acc + low[i, k] * inv[k, c]
                    inv[i, c] = -(acc * root)
            sums = [None] * (2 * n // LANES)
            for c in range(TILE):
                column = jnp.where(sub == c, inv[c, c], 0.0)
                for r in range(c + 1, TILE):
                    column = jnp.where(sub == r, inv[r, c], column)
                for k in range(len(sums)):
                    term = column * rows[c : c + 1, k * LANES : (k + 1) * LANES]
                    sums[k] = term if sums[k] is None else sums[k] + term
            rows = jnp.concatenate(sums, axis=1)
            work[pl.ds(start, TILE), :] = rows
            update = transposed_by(rows[:, base : base + size], rows)
            below = in_panel > start + (TILE - 1) - base
            work[base : base + size, :] = work[base : base + size, :] - jnp.where(
                below, update, 0.0
            )
            return carry

        lax.fori_loop(first, last, block, 0)
        end = base + size
        if last * TILE == end and end < n:
            done = work[base:end, :]
            work[end:, :] = work[end:, :] - transposed_by(done[:, end:n], done)

    def inverse(self):
        return self.work[:, self.n :]


def step_kernel(shape, momentum, gradient, basis, ortho_out, factor_out, rms_out, mem, sent, wire):
    reps, cols, depth, m, n, sub, rank, order = shape
    row = lax.axis_index("row")
    core = lax.rem(row, CORES)
    z, y, x = lax.div(row, CORES), lax.axis_index("col"), lax.axis_index("rep")
    half = rank // CORES
    part_x, part_xy, part_z = m // reps, m // reps // cols, sub // depth
    part_g = rank // (reps * cols)
    axes = {
        "x": (reps, x, lambda p: {"rep": p}),
        "y": (cols, y, lambda p: {"col": p}),
        "z": (depth, z, lambda p: {"row": p * CORES + core}),
        "c": (CORES, core, lambda p: {"row": z * CORES + p}),
    }
    used = [0]
    pending = []

    def send(axis, source, target, me_slot):
        size, me, device = axes[axis]
        first = used[0]
        used[0] += size - 1
        for i in range(1, size):
            peer = lax.rem(me + i, size)
            copy = pltpu.make_async_remote_copy(
                src_ref=source(peer),
                dst_ref=target(me_slot),
                send_sem=sent.at[first + i - 1],
                recv_sem=wire.at[first + i - 1],
                device_id=device(peer),
                device_id_type=MESH,
            )
            copy.start()
            pending.append(copy)

        def wait():
            for i in range(1, size):
                origin = lax.rem(me + size - i, size)
                pltpu.make_async_remote_copy(
                    src_ref=source(origin),
                    dst_ref=target(origin),
                    send_sem=sent.at[first + i - 1],
                    recv_sem=wire.at[first + i - 1],
                    device_id=device(origin),
                    device_id_type=MESH,
                ).wait_recv()

        return wait

    barrier = pltpu.get_barrier_semaphore()
    partners = 0
    for size, me, device in axes.values():
        for i in range(1, size):
            pl.semaphore_signal(
                barrier, inc=1, device_id=device(lax.rem(me + i, size)), device_id_type=MESH
            )
            partners += 1

    product = None
    for k in range(reps):
        lanes = slice(k * sub, (k + 1) * sub)
        mem["piece"][k] = momentum[0, :, lanes] + gradient[0, :, lanes].astype(jnp.float32)
        term = rows_by_rows(mem["piece"][k], basis[lanes, :])
        product = term if product is None else product + term
    mem["left_part"][0] = product * (1.0 / reps)
    pl.semaphore_wait(barrier, partners)

    def reduce_left(it):
        part, from_x, from_y = mem["left_part"].at[it], mem["left_x"].at[it], mem["left_y"].at[it]
        all_y, all_x = mem["left_gy"].at[it], mem["left_gx"].at[it]

        def rows_of(p):
            return pl.ds(pl.multiple_of(p * part_x, TILE), part_x)

        wait = send("x", lambda p: part.at[rows_of(p), :], lambda s: from_x.at[s], x)
        from_x[x] = part[rows_of(x), :]
        yield
        wait()
        total = from_x[0]
        for s in range(1, reps):
            total = total + from_x[s]
        mid = mem["left_mid"].at[it]
        mid[...] = total.reshape(cols, part_xy, rank)
        wait = send("y", lambda p: mid.at[p], lambda s: from_y.at[s], y)
        from_y[y] = mid[y]
        yield
        wait()
        total = from_y[0]
        for s in range(1, cols):
            total = total + from_y[s]
        all_y[y] = total
        wait = send("y", lambda p: all_y.at[y], lambda s: all_y.at[s], y)
        yield
        wait()
        all_x[x] = all_y[...]
        wait = send("x", lambda p: all_y, lambda s: all_x.at[s], x)
        yield
        wait()

    def run(stages, fillers=()):
        fillers = list(fillers)
        for number, _ in enumerate(stages):
            if number < len(fillers):
                fillers[number]()

    def left_of(it):
        return mem["left_gx"][it].reshape(m, rank)

    stages = reduce_left(0)
    next(stages)
    exchange = send("x", lambda p: mem["piece"].at[p], lambda s: mem["pieces"].at[s], x)
    mem["pieces"][x] = mem["piece"][x]
    run(stages)
    exchange()
    total = mem["pieces"][0]
    for s in range(1, reps):
        total = total + mem["pieces"][s]
    mem["mean"][...] = total * (1.0 / reps)

    def reduce_right(it, left):
        partial = transposed_by(mem["mean"][...], left)
        mem["gram_part"][it] = transposed_by(left, left)
        mine = pl.multiple_of((x * cols + y) * part_g, TILE)
        gram = mem["gram_part"][it, pl.ds(mine, part_g), :]
        split, other = mem["right_split"].at[it], mem["right_core"].at[it]
        for h in range(CORES):
            lanes = slice(h * half, (h + 1) * half)
            split[h, :sub, :] = partial[:, lanes]
            split[h, sub:, :] = gram[:, lanes]
        wait = send("c", lambda p: split.at[p], lambda s: other.at[0], 0)
        wait()
        both = split[core] + other[0]
        out, got = mem["right_z"].at[it], mem["right_fz"].at[it]
        for s in range(depth):
            out[s, :part_z, :] = both[s * part_z : (s + 1) * part_z, :]
            out[s, part_z:, :] = both[sub:, :]
        wait = send("z", lambda p: out.at[p], lambda s: got.at[s], z)
        got[z] = out[z]
        yield
        wait()
        total = got[0]
        for s in range(1, depth):
            total = total + got[s]
        full, by_y, by_x = mem["right"].at[it], mem["gram_y"].at[it], mem["gram"].at[it]
        full[core, z] = total[:part_z, :]
        wait_z = send("z", lambda p: full.at[core, z], lambda s: full.at[core, s], z)
        by_y[y] = total[part_z:, :]
        wait_y = send("y", lambda p: by_y.at[y], lambda s: by_y.at[s], y)
        yield
        wait_y()
        by_x[core, x] = by_y[...]
        wait_x = send("x", lambda p: by_x.at[core, x], lambda s: by_x.at[core, s], x)
        wait_z()
        wait_c = send("c", lambda p: full.at[core], lambda s: full.at[s], core)
        wait_x()
        wait_g = send("c", lambda p: by_x.at[core], lambda s: by_x.at[s], core)
        yield
        wait_c()
        yield
        wait_g()

    def right_of(it):
        return jnp.concatenate(
            [mem["right"][it, h].reshape(sub, half) for h in range(CORES)], axis=1
        )

    def gram_of(it):
        return jnp.concatenate(
            [mem["gram"][it, h].reshape(rank, half) for h in range(CORES)], axis=1
        )

    def root_mean(it, factor):
        by_x, by_y = mem["square_x"].at[it], mem["square_y"].at[it]
        squares = jnp.sum(factor * factor, axis=0, keepdims=True)
        by_x[x] = jnp.broadcast_to(squares, (TILE, rank))
        wait = send("x", lambda p: by_x.at[x], lambda s: by_x.at[s], x)
        yield
        wait()
        total = by_x[0]
        for s in range(1, reps):
            total = total + by_x[s]
        by_y[y] = total
        wait = send("y", lambda p: by_y.at[y], lambda s: by_y.at[s], y)
        yield
        wait()
        total = by_y[0]
        for s in range(1, cols):
            total = total + by_y[s]
        mem["rms"][it] = jnp.sqrt(total / jnp.float32(order) + 1e-06)

    chol = Cholesky(mem["chol"])
    blocks = rank // TILE

    def some(first, last):
        return functools.partial(chol.blocks, first, last)

    stages = reduce_right(0, left_of(0))
    next(stages)
    next(stages)
    next(stages)
    next(stages)
    right = right_of(0)
    mem["left_part"][1] = rows_by_rows(mem["mean"][...], right)
    for _ in stages:
        pass
    stages_left = reduce_left(1)
    next(stages_left)
    chol.load(gram_of(0))
    quarter = blocks // 4
    some(0, quarter)()
    next(stages_left)
    some(quarter, 2 * quarter)()
    next(stages_left)
    some(2 * quarter, 3 * quarter)()
    next(stages_left)
    some(3 * quarter, blocks)()
    inverse = chol.inverse()
    squares = root_mean(0, by_transposed(right, inverse))
    next(squares)
    for _ in stages_left:
        pass
    left = by_transposed(left_of(1), inverse)
    next(squares)

    stages = reduce_right(1, left)
    next(stages)
    for _ in squares:
        pass
    scale = 1.0 / mem["rms"][0]
    next(stages)
    next(stages)
    next(stages)
    right = right_of(1) * scale[:1, :]
    for _ in stages:
        pass
    mem["scale"][...] = scale
    across = jnp.transpose(jnp.broadcast_to(scale[:1, :], (LANES, rank)))[:, :1]
    chol.load(gram_of(1) * scale[:1, :] * across)
    for i in range(4):
        some(i * quarter, (i + 1) * quarter)()
    inverse = chol.inverse()
    factor = by_transposed(right, inverse)
    mem["factor"][x] = factor
    wait = send("x", lambda p: mem["factor"].at[x], lambda s: mem["factor"].at[s], x)
    squares = root_mean(1, factor)
    next(squares)
    ortho_out[...] = by_transposed(left * mem["scale"][:1, :], inverse)
    next(squares)
    for _ in squares:
        pass
    rms_out[...] = mem["rms"][1]
    wait()
    for k in range(reps):
        factor_out[k * sub : (k + 1) * sub, :] = mem["factor"][k]
    for copy in pending:
        copy.wait_send()
    assert used[0] == sent.shape[0]


def step(mesh, momentum, gradient, weight, right_basis):
    reps, cols = mesh.shape["rep"], mesh.shape["col"]
    depth = mesh.shape["row"] // CORES
    _, m, n = momentum.shape
    sub, rank = n // reps, right_basis.shape[1]
    order = n * cols
    half = rank // CORES
    part_x, part_xy, part_z = m // reps, m // reps // cols, sub // depth
    part_g = rank // (reps * cols)
    f32 = jnp.float32
    shapes = {
        "piece": (reps, m, sub),
        "pieces": (reps, m, sub),
        "mean": (m, sub),
        "left_part": (2, m, rank),
        "left_x": (2, reps, part_x, rank),
        "left_mid": (2, cols, part_xy, rank),
        "left_y": (2, cols, part_xy, rank),
        "left_gy": (2, cols, part_xy, rank),
        "left_gx": (2, reps, cols, part_xy, rank),
        "gram_part": (2, rank, rank),
        "right_split": (2, CORES, sub + part_g, half),
        "right_core": (2, 1, sub + part_g, half),
        "right_z": (2, depth, part_z + part_g, half),
        "right_fz": (2, depth, part_z + part_g, half),
        "right": (2, CORES, depth, part_z, half),
        "gram_y": (2, cols, part_g, half),
        "gram": (2, CORES, reps, cols, part_g, half),
        "square_x": (2, reps, TILE, rank),
        "square_y": (2, cols, TILE, rank),
        "rms": (2, TILE, rank),
        "scale": (TILE, rank),
        "chol": (rank, 2 * rank),
        "factor": (reps, sub, rank),
    }
    links = {"x": reps - 1, "y": cols - 1, "z": depth - 1, "c": CORES - 1}
    left_links = 2 * links["x"] + 2 * links["y"]
    right_links = 2 * links["z"] + links["y"] + links["x"] + 3 * links["c"]
    copies = 2 * (left_links + right_links + links["x"] + links["y"]) + 2 * links["x"]
    vmem = pl.BlockSpec(memory_space=pltpu.VMEM)
    ortho, factor, rms = pl.pallas_call(
        functools.partial(step_kernel, (reps, cols, depth, m, n, sub, rank, order)),
        out_shape=[
            jax.ShapeDtypeStruct((m, rank), f32),
            jax.ShapeDtypeStruct((n, rank), f32),
            jax.ShapeDtypeStruct((TILE, rank), f32),
        ],
        in_specs=[vmem] * 3,
        out_specs=[vmem] * 3,
        scratch_shapes=[
            {name: pltpu.VMEM(dims, f32) for name, dims in shapes.items()},
            pltpu.SemaphoreType.DMA((copies,)),
            pltpu.SemaphoreType.DMA((copies,)),
        ],
        compiler_params=pltpu.CompilerParams(
            collective_id=0, has_side_effects=True, vmem_limit_bytes=40 << 20
        ),
        name="dion_step",
    )(momentum, gradient, right_basis)
    highest = lax.Precision.HIGHEST
    buffer = momentum[0] + gradient[0].astype(f32)
    new_basis = factor / rms[:1, :]
    feedback = jnp.dot(ortho, factor.T, precision=highest, preferred_element_type=f32)
    new_momentum = (buffer - (1.0 - beta_mom) * feedback)[None]
    update = jnp.dot(ortho, new_basis.T, precision=highest, preferred_element_type=f32)
    new_weight = weight - learn_rate * jnp.sqrt(f32(order) / f32(rank)) * update
    return new_momentum, new_weight, new_basis


def solution(mesh):
    return jax.shard_map(
        functools.partial(step, mesh),
        mesh=mesh,
        in_specs=(P("rep", "row", "col"), P("rep", "row", "col"), P("row", "col"), P("col", None)),
        out_specs=(P("rep", "row", "col"), P("row", "col"), P("col", None)),
        check_vma=False,
    )
```

```python
import functools

import jax
import jax.numpy as jnp
from jax import lax
from jax.experimental import pallas as pl
from jax.experimental.pallas import tpu as pltpu
from jax.sharding import PartitionSpec as P

beta_mom = 0.95
learn_rate = 0.05
CORES = 2
TILE = 8
LANES = 128
HIGHEST = lax.Precision.HIGHEST
MESH = pl.DeviceIdType.MESH


def dot(a, b, over):
    return lax.dot_general(
        a, b, (over, ((), ())), precision=HIGHEST, preferred_element_type=jnp.float32
    )


def rows_by_rows(a, b):
    return dot(a, b, ((1,), (0,)))


def by_transposed(a, b):
    return dot(a, b, ((1,), (1,)))


def transposed_by(a, b):
    return dot(a, b, ((0,), (0,)))


def in_three(x):
    high = x.astype(jnp.bfloat16).astype(jnp.float32)
    rest = x - high
    middle = rest.astype(jnp.bfloat16).astype(jnp.float32)
    return high, middle, rest - middle


def thin_product(a, b):
    (ah, am, al), (bh, bm, bl) = in_three(a), in_three(b)
    left = jnp.concatenate([ah, ah, am, am, ah, al], axis=0).astype(jnp.bfloat16)
    right = jnp.concatenate([bh, bm, bh, bm, bl, bh], axis=0).astype(jnp.bfloat16)
    return lax.dot_general(
        left, right, (((0,), (0,)), ((), ())), preferred_element_type=jnp.float32
    )


class Cholesky:
    group = 4

    def __init__(self, work):
        self.work = work
        self.n = work.shape[0]
        self.panel = min(128, self.n)
        self.groups = self.n // (TILE * self.group)

    def load(self, gram):
        n = self.n
        self.work[:, :n] = gram
        eye = lax.broadcasted_iota(jnp.int32, (n, n), 0) == lax.broadcasted_iota(
            jnp.int32, (n, n), 1
        )
        self.work[:, n:] = jnp.where(eye, 1.0, 0.0)

    def run(self, first, last):
        work, n, size, count = self.work, self.n, self.panel, self.group
        step = TILE * count
        base = (first * step // size) * size
        wide = (TILE, LANES)
        tiles = 2 * n // LANES
        sub = lax.broadcasted_iota(jnp.int32, wide, 0)
        in_panel = lax.broadcasted_iota(jnp.int32, (size, 1), 0)

        def spread(block, lane):
            return jnp.broadcast_to(block[:, lane : lane + 1], wide)

        def body(t, carry):
            start = pl.multiple_of(t * step, step)
            rows, small = [], []
            for b in range(count):
                got = work[pl.ds(start + TILE * b, TILE), :]
                rows.append([got[:, k * LANES : (k + 1) * LANES] for k in range(tiles)])
                small.append(pltpu.roll(got[:, :n], lax.rem(n - start, n), 1)[:, :LANES])
            for b in range(count):
                columns = [spread(small[b], TILE * b + i) for i in range(TILE)]
                below = {
                    c: [spread(small[c], TILE * b + i) for i in range(TILE)]
                    for c in range(b + 1, count)
                }
                a = {
                    (r, i): jnp.broadcast_to(columns[i][r : r + 1, :], wide)
                    for i in range(TILE)
                    for r in range(i, TILE)
                }
                low, inv = {}, {}
                for i in range(TILE):
                    root = lax.rsqrt(a[i, i])
                    inv[i, i] = root
                    for r in range(i + 1, TILE):
                        low[r, i] = a[r, i] * root
                    for r in range(i + 1, TILE):
                        for c in range(i + 1, r + 1):
                            a[r, c] = a[r, c] - low[r, i] * low[c, i]
                    for c in range(i):
                        acc = low[i, c] * inv[c, c]
                        for k in range(c + 1, i):
                            acc = acc + low[i, k] * inv[k, c]
                        inv[i, c] = -(acc * root)
                sums = [None] * (tiles + 1)
                source = rows[b] + [small[b]]
                for c in range(TILE):
                    column = jnp.where(sub == c, inv[c, c], 0.0)
                    for r in range(c + 1, TILE):
                        column = jnp.where(sub == r, inv[r, c], column)
                    for k in range(tiles + 1):
                        term = column * source[k][c : c + 1, :]
                        sums[k] = term if sums[k] is None else sums[k] + term
                rows[b], small[b] = sums[:tiles], sums[tiles]
                for c in range(b + 1, count):
                    for i in range(TILE):
                        lower = below[c][0] * inv[i, 0]
                        for k in range(1, i + 1):
                            lower = lower + below[c][k] * inv[i, k]
                        rows[c] = [rows[c][k] - lower * rows[b][k][i : i + 1, :] for k in range(tiles)]
                        small[c] = small[c] - lower * small[b][i : i + 1, :]
            done = jnp.concatenate([jnp.concatenate(r, axis=1) for r in rows], axis=0)
            work[pl.ds(start, step), :] = done
            update = thin_product(done[:, base : base + size], done)
            keep = in_panel > start + (step - 1) - base
            work[base : base + size, :] = work[base : base + size, :] - jnp.where(keep, update, 0.0)
            return carry

        lax.fori_loop(first, last, body, 0)
        end = base + size
        if last * step == end and end < n:
            done = work[base:end, :]
            work[end:, :] = work[end:, :] - transposed_by(done[:, end:n], done)

    def inverse(self):
        return self.work[:, self.n :]


def step_kernel(shape, momentum_in, gradient_in, basis_in, ortho_out, factor_out, rms_out, mem, gradient, local, sent, wire):
    reps, cols, depth, m, n, sub, rank, order = shape
    row = lax.axis_index("row")
    core = lax.rem(row, CORES)
    z, y, x = lax.div(row, CORES), lax.axis_index("col"), lax.axis_index("rep")
    plane = reps * cols
    here = x * cols + y
    half = rank // CORES
    part, part_z, part_g = m // plane, sub // depth, rank // plane

    def far_first(size):
        return sorted(range(1, size), key=lambda i: -min(i, size - i))

    def line(size, me, device):
        return [
            (lax.rem(me + i, size), lax.rem(me + size - i, size), device(lax.rem(me + i, size)))
            for i in far_first(size)
        ]

    def sheet():
        pairs = [(i, j) for i in range(reps) for j in range(cols) if i or j]
        pairs.sort(key=lambda p: -(min(p[0], reps - p[0]) + min(p[1], cols - p[1])))
        out = []
        for i, j in pairs:
            px, py = lax.rem(x + i, reps), lax.rem(y + j, cols)
            ox, oy = lax.rem(x + reps - i, reps), lax.rem(y + cols - j, cols)
            out.append((px * cols + py, ox * cols + oy, {"rep": px, "col": py}))
        return out

    groups = {
        "x": line(reps, x, lambda p: {"rep": p}),
        "y": line(cols, y, lambda p: {"col": p}),
        "z": line(depth, z, lambda p: {"row": p * CORES + core}),
        "c": line(CORES, core, lambda p: {"row": z * CORES + p}),
        "xy": sheet(),
    }
    used = [0]
    pending = []

    def send(group, source, target, mine):
        first = used[0]
        members = groups[group]
        used[0] += len(members)
        for i, (peer, origin, device) in enumerate(members):
            copy = pltpu.make_async_remote_copy(
                src_ref=source(peer),
                dst_ref=target(mine),
                send_sem=sent.at[first + i],
                recv_sem=wire.at[first + i],
                device_id=device,
                device_id_type=MESH,
            )
            copy.start()
            pending.append(copy)

        def wait():
            for i, (peer, origin, device) in enumerate(members):
                pltpu.make_async_remote_copy(
                    src_ref=source(origin),
                    dst_ref=target(origin),
                    send_sem=sent.at[first + i],
                    recv_sem=wire.at[first + i],
                    device_id=device,
                    device_id_type=MESH,
                ).wait_recv()

        return wait

    loads = [
        pltpu.make_async_copy(momentum_in.at[0], mem["momentum"], local.at[0]),
        pltpu.make_async_copy(gradient_in.at[0], gradient, local.at[1]),
        pltpu.make_async_copy(basis_in, mem["basis"], local.at[2]),
    ]
    for load in loads:
        load.start()
    barrier = pltpu.get_barrier_semaphore()
    partners = 0
    for group in ("z", "xy", "c"):
        for _, _, device in groups[group]:
            pl.semaphore_signal(barrier, inc=1, device_id=device, device_id_type=MESH)
            partners += 1
    for load in loads:
        load.wait()

    product = None
    for k in range(reps):
        lanes = slice(k * sub, (k + 1) * sub)
        mem["piece"][k] = mem["momentum"][:, lanes] + gradient[:, lanes].astype(jnp.float32)
        term = rows_by_rows(mem["piece"][k], mem["basis"][lanes, :])
        product = term if product is None else product + term

    def added(ref):
        total = ref[0]
        for s in range(1, ref.shape[0]):
            total = total + ref[s]
        return total

    def scatter_left(it, partial):
        out, got = mem["left_part"].at[it], mem["left_got"].at[it]
        out[...] = partial.reshape(plane, part, rank)
        wait = send("xy", lambda p: out.at[p], lambda s: got.at[s], here)
        got[here] = out[here]
        return wait

    def gather_left(it):
        full = mem["left"].at[it]
        full[here] = added(mem["left_got"].at[it])
        return send("xy", lambda p: full.at[here], lambda s: full.at[s], here)

    def left_of(it):
        return mem["left"][it].reshape(m, rank)

    def reduce_right(it):
        now = mem["now"]
        split, other = mem["right_split"].at[it], mem["right_core"].at[it]
        sibling = CORES - 1 - core

        def lanes_of(h):
            return pl.ds(pl.multiple_of(h * half, half), half)

        mean_t = mem["mean_t"][...]
        split[0] = rows_by_rows(mean_t, now[:, lanes_of(sibling)])
        wait_c = send("c", lambda p: split.at[0], lambda s: other.at[0], 0)
        split[1] = rows_by_rows(mean_t, now[:, lanes_of(core)])
        mem["gram_part"][it] = transposed_by(now[...], now[...])
        mine = pl.ds(pl.multiple_of(here * part_g, TILE), part_g)
        g_out, g_other = mem["gram_split"].at[it], mem["gram_core"].at[it]
        g_out[...] = mem["gram_part"][it, mine, lanes_of(sibling)]
        wait_g = send("c", lambda p: g_out, lambda s: g_other, 0)
        wait_c()
        out, got = mem["right_z"].at[it], mem["right_got"].at[it]
        out[...] = (split[1] + other[0]).reshape(depth, part_z, half)
        wait_c = send("z", lambda p: out.at[p], lambda s: got.at[s], z)
        got[z] = out[z]
        wait_g()
        g_all = mem["gram_z"].at[it]
        g_all[z] = mem["gram_part"][it, mine, lanes_of(core)] + g_other[...]
        wait_g = send("z", lambda p: g_all.at[z], lambda s: g_all.at[s], z)
        yield
        wait_c()
        full = mem["right"].at[it]
        full[core, z] = added(got)
        wait_c = send("z", lambda p: full.at[core, z], lambda s: full.at[core, s], z)
        wait_g()
        gram = mem["gram"].at[it]
        gram[core, here] = added(g_all)
        wait_g = send("xy", lambda p: gram.at[core, here], lambda s: gram.at[core, s], here)
        yield
        wait_c()
        wait_c = send("c", lambda p: full.at[core], lambda s: full.at[s], core)
        wait_g()
        wait_g = send("c", lambda p: gram.at[core], lambda s: gram.at[s], core)
        wait_c()
        yield
        wait_g()

    def joined(ref, rows):
        return jnp.concatenate([ref[h].reshape(rows, half) for h in range(CORES)], axis=1)

    def squares_of(factor):
        squares = jnp.sum(factor * factor, axis=0, keepdims=True)
        return jnp.broadcast_to(squares, (TILE, rank))

    def share(group, name, mine, value):
        ref = mem[name]
        ref[mine] = value
        return send(group, lambda p: ref.at[mine], lambda s: ref.at[s], mine)

    def rms_of(total):
        return jnp.sqrt(total / jnp.float32(order) + 1e-06)

    chol = Cholesky(mem["chol"])
    middle = chol.groups // 2

    pl.semaphore_wait(barrier, partners)
    wait_left = scatter_left(0, product * (1.0 / reps))
    exchange = send("x", lambda p: mem["piece"].at[p], lambda s: mem["pieces"].at[s], x)
    mem["pieces"][x] = mem["piece"][x]
    wait_left()
    wait_left = gather_left(0)
    exchange()
    mem["mean"][...] = added(mem["pieces"]) * (1.0 / reps)
    mem["mean_t"][...] = jnp.transpose(mem["mean"][...])
    wait_left()

    mem["now"][...] = left_of(0)
    stages = reduce_right(0)
    next(stages)
    next(stages)
    next(stages)
    right = joined(mem["right"].at[0], sub)
    wait_left = scatter_left(1, rows_by_rows(mem["mean"][...], right))
    for _ in stages:
        pass
    chol.load(joined(mem["gram"].at[0], rank))
    chol.run(0, middle)
    wait_left()
    wait_left = gather_left(1)
    chol.run(middle, chol.groups)
    inverse = chol.inverse()
    wait_left()
    left = by_transposed(left_of(1), inverse)
    mem["now"][...] = left

    stages = reduce_right(1)
    next(stages)
    squares = squares_of(by_transposed(joined(mem["right"].at[0], sub), inverse))
    wait_squares = share("x", "square_x", x, squares)
    next(stages)
    wait_squares()
    wait_squares = share("y", "square_y", y, added(mem["square_x"]))
    next(stages)
    gathered = mem["rights"]
    gathered[x] = mem["right"][1]
    wait_right = send("x", lambda p: mem["right"].at[1], lambda s: gathered.at[s], x)
    wait_squares()
    scale = (1.0 / rms_of(added(mem["square_y"])))[:1, :]
    mem["scale"][...] = jnp.broadcast_to(scale, (TILE, rank))
    across = jnp.transpose(jnp.broadcast_to(scale, (LANES, rank)))[:, :1]
    for _ in stages:
        pass
    chol.load(joined(mem["gram"].at[1], rank) * scale * across)
    chol.run(0, middle)
    chol.run(middle, chol.groups)
    inverse = chol.inverse()
    scale = mem["scale"][:1, :]
    wait_right()
    squares = None
    for k in range(reps):
        factor = by_transposed(joined(gathered.at[k], sub) * scale, inverse)
        factor_out[k * sub : (k + 1) * sub, :] = factor
        term = squares_of(factor)
        squares = term if squares is None else squares + term
    wait_squares = share("y", "square_last", y, squares)
    ortho_out[...] = by_transposed(mem["now"][...] * scale, inverse)
    for copy in pending:
        copy.wait_send()
    wait_squares()
    rms_out[...] = rms_of(added(mem["square_last"]))
    assert used[0] == sent.shape[0]


def step(mesh, momentum, gradient, weight, right_basis):
    reps, cols = mesh.shape["rep"], mesh.shape["col"]
    depth = mesh.shape["row"] // CORES
    _, m, n = momentum.shape
    sub, rank = n // reps, right_basis.shape[1]
    order = n * cols
    half, plane = rank // CORES, reps * cols
    part, part_z, part_g = m // plane, sub // depth, rank // plane
    f32 = jnp.float32
    shapes = {
        "momentum": (m, n),
        "basis": (n, rank),
        "piece": (reps, m, sub),
        "pieces": (reps, m, sub),
        "mean": (m, sub),
        "mean_t": (sub, m),
        "left_part": (2, plane, part, rank),
        "left_got": (2, plane, part, rank),
        "left": (2, plane, part, rank),
        "now": (m, rank),
        "gram_part": (2, rank, rank),
        "right_split": (2, CORES, sub, half),
        "right_core": (2, 1, sub, half),
        "gram_split": (2, part_g, half),
        "gram_core": (2, part_g, half),
        "right_z": (2, depth, part_z, half),
        "right_got": (2, depth, part_z, half),
        "right": (2, CORES, depth, part_z, half),
        "gram_z": (2, depth, part_g, half),
        "gram": (2, CORES, plane, part_g, half),
        "square_x": (reps, TILE, rank),
        "square_y": (cols, TILE, rank),
        "square_last": (cols, TILE, rank),
        "scale": (TILE, rank),
        "chol": (rank, 2 * rank),
        "rights": (reps, CORES, depth, part_z, half),
    }
    links = {"x": reps - 1, "y": cols - 1, "z": depth - 1, "c": CORES - 1, "xy": plane - 1}
    copies = 2 * (3 * links["xy"] + 3 * links["z"] + 4 * links["c"] + links["x"] + links["y"])
    copies += links["x"]
    hbm = pl.BlockSpec(memory_space=pl.ANY)
    vmem = pl.BlockSpec(memory_space=pltpu.VMEM)
    ortho, factor, rms = pl.pallas_call(
        functools.partial(step_kernel, (reps, cols, depth, m, n, sub, rank, order)),
        out_shape=[
            jax.ShapeDtypeStruct((m, rank), f32),
            jax.ShapeDtypeStruct((n, rank), f32),
            jax.ShapeDtypeStruct((TILE, rank), f32),
        ],
        in_specs=[hbm] * 3,
        out_specs=[vmem] * 3,
        scratch_shapes=[
            {name: pltpu.VMEM(dims, f32) for name, dims in shapes.items()},
            pltpu.VMEM((m, n), gradient.dtype),
            pltpu.SemaphoreType.DMA((3,)),
            pltpu.SemaphoreType.DMA((copies,)),
            pltpu.SemaphoreType.DMA((copies,)),
        ],
        compiler_params=pltpu.CompilerParams(
            collective_id=0, has_side_effects=True, vmem_limit_bytes=58 << 20
        ),
        name="dion_step",
    )(momentum, gradient, right_basis)
    highest = lax.Precision.HIGHEST
    buffer = momentum[0] + gradient[0].astype(f32)
    new_basis = factor / rms[:1, :]
    feedback = jnp.dot(ortho, factor.T, precision=highest, preferred_element_type=f32)
    new_momentum = (buffer - (1.0 - beta_mom) * feedback)[None]
    update = jnp.dot(ortho, new_basis.T, precision=highest, preferred_element_type=f32)
    new_weight = weight - learn_rate * jnp.sqrt(f32(order) / f32(rank)) * update
    return new_momentum, new_weight, new_basis


def solution(mesh):
    return jax.shard_map(
        functools.partial(step, mesh),
        mesh=mesh,
        in_specs=(P("rep", "row", "col"), P("rep", "row", "col"), P("row", "col"), P("col", None)),
        out_specs=(P("rep", "row", "col"), P("row", "col"), P("col", None)),
        check_vma=False,
    )
```

```python
import functools

import jax
import jax.numpy as jnp
from jax import lax
from jax.experimental import pallas as pl
from jax.experimental.pallas import tpu as pltpu
from jax.sharding import PartitionSpec as P

beta_mom = 0.95
learn_rate = 0.05
CORES = 2
TILE = 8
LANES = 128
HIGHEST = lax.Precision.HIGHEST
MESH = pl.DeviceIdType.MESH


def dot(a, b, over):
    return lax.dot_general(
        a, b, (over, ((), ())), precision=HIGHEST, preferred_element_type=jnp.float32
    )


def rows_by_rows(a, b):
    return dot(a, b, ((1,), (0,)))


def by_transposed(a, b):
    return dot(a, b, ((1,), (1,)))


def transposed_by(a, b):
    return dot(a, b, ((0,), (0,)))


def in_three(x):
    high = x.astype(jnp.bfloat16).astype(jnp.float32)
    rest = x - high
    middle = rest.astype(jnp.bfloat16).astype(jnp.float32)
    return high, middle, rest - middle


def thin_product(a, b):
    (ah, am, al), (bh, bm, bl) = in_three(a), in_three(b)
    left = jnp.concatenate([ah, ah, am, am, ah, al], axis=0).astype(jnp.bfloat16)
    right = jnp.concatenate([bh, bm, bh, bm, bl, bh], axis=0).astype(jnp.bfloat16)
    return lax.dot_general(
        left, right, (((0,), (0,)), ((), ())), preferred_element_type=jnp.float32
    )


class Cholesky:
    group = 4

    def __init__(self, work):
        self.work = work
        self.n = work.shape[0]
        self.panel = min(128, self.n)
        self.groups = self.n // (TILE * self.group)

    def load(self, gram):
        n = self.n
        self.work[:, :n] = gram
        eye = lax.broadcasted_iota(jnp.int32, (n, n), 0) == lax.broadcasted_iota(
            jnp.int32, (n, n), 1
        )
        self.work[:, n:] = jnp.where(eye, 1.0, 0.0)

    def run(self, first, last):
        work, n, size, count = self.work, self.n, self.panel, self.group
        step = TILE * count
        base = (first * step // size) * size
        wide = (TILE, LANES)
        tiles = 2 * n // LANES
        sub = lax.broadcasted_iota(jnp.int32, wide, 0)
        in_panel = lax.broadcasted_iota(jnp.int32, (size, 1), 0)

        def spread(block, lane):
            return jnp.broadcast_to(block[:, lane : lane + 1], wide)

        def body(t, carry):
            start = pl.multiple_of(t * step, step)
            rows, small = [], []
            for b in range(count):
                got = work[pl.ds(start + TILE * b, TILE), :]
                rows.append([got[:, k * LANES : (k + 1) * LANES] for k in range(tiles)])
                small.append(pltpu.roll(got[:, :n], lax.rem(n - start, n), 1)[:, :LANES])
            for b in range(count):
                columns = [spread(small[b], TILE * b + i) for i in range(TILE)]
                below = {
                    c: [spread(small[c], TILE * b + i) for i in range(TILE)]
                    for c in range(b + 1, count)
                }
                a = {
                    (r, i): jnp.broadcast_to(columns[i][r : r + 1, :], wide)
                    for i in range(TILE)
                    for r in range(i, TILE)
                }
                low, inv = {}, {}
                for i in range(TILE):
                    root = lax.rsqrt(a[i, i])
                    inv[i, i] = root
                    for r in range(i + 1, TILE):
                        low[r, i] = a[r, i] * root
                    for r in range(i + 1, TILE):
                        for c in range(i + 1, r + 1):
                            a[r, c] = a[r, c] - low[r, i] * low[c, i]
                    for c in range(i):
                        acc = low[i, c] * inv[c, c]
                        for k in range(c + 1, i):
                            acc = acc + low[i, k] * inv[k, c]
                        inv[i, c] = -(acc * root)
                sums = [None] * (tiles + 1)
                source = rows[b] + [small[b]]
                for c in range(TILE):
                    column = jnp.where(sub == c, inv[c, c], 0.0)
                    for r in range(c + 1, TILE):
                        column = jnp.where(sub == r, inv[r, c], column)
                    for k in range(tiles + 1):
                        term = column * source[k][c : c + 1, :]
                        sums[k] = term if sums[k] is None else sums[k] + term
                rows[b], small[b] = sums[:tiles], sums[tiles]
                for c in range(b + 1, count):
                    for i in range(TILE):
                        lower = below[c][0] * inv[i, 0]
                        for k in range(1, i + 1):
                            lower = lower + below[c][k] * inv[i, k]
                        rows[c] = [rows[c][k] - lower * rows[b][k][i : i + 1, :] for k in range(tiles)]
                        small[c] = small[c] - lower * small[b][i : i + 1, :]
            done = jnp.concatenate([jnp.concatenate(r, axis=1) for r in rows], axis=0)
            work[pl.ds(start, step), :] = done
            update = thin_product(done[:, base : base + size], done)
            keep = in_panel > start + (step - 1) - base
            work[base : base + size, :] = work[base : base + size, :] - jnp.where(keep, update, 0.0)
            return carry

        lax.fori_loop(first, last, body, 0)
        end = base + size
        if last * step == end and end < n:
            done = work[base:end, :]
            work[end:, :] = work[end:, :] - transposed_by(done[:, end:n], done)

    def inverse(self):
        return self.work[:, self.n :]


def step_kernel(shape, momentum_in, gradient_in, basis_in, ortho_out, factor_out, rms_out, mem, gradient, local, sent, wire):
    reps, cols, depth, m, n, sub, rank, order = shape
    row = lax.axis_index("row")
    core = lax.rem(row, CORES)
    z, y, x = lax.div(row, CORES), lax.axis_index("col"), lax.axis_index("rep")
    plane = reps * cols
    here = x * cols + y
    half = rank // CORES
    part, part_z, part_g = m // plane, sub // depth, rank // plane

    def far_first(size):
        return sorted(range(1, size), key=lambda i: -min(i, size - i))

    def line(size, me, device):
        return [
            (lax.rem(me + i, size), lax.rem(me + size - i, size), device(lax.rem(me + i, size)))
            for i in far_first(size)
        ]

    def sheet():
        pairs = [(i, j) for i in range(reps) for j in range(cols) if i or j]
        pairs.sort(key=lambda p: -(min(p[0], reps - p[0]) + min(p[1], cols - p[1])))
        out = []
        for i, j in pairs:
            px, py = lax.rem(x + i, reps), lax.rem(y + j, cols)
            ox, oy = lax.rem(x + reps - i, reps), lax.rem(y + cols - j, cols)
            out.append((px * cols + py, ox * cols + oy, {"rep": px, "col": py}))
        return out

    groups = {
        "x": line(reps, x, lambda p: {"rep": p}),
        "y": line(cols, y, lambda p: {"col": p}),
        "z": line(depth, z, lambda p: {"row": p * CORES + core}),
        "c": line(CORES, core, lambda p: {"row": z * CORES + p}),
        "xy": sheet(),
    }
    used = [0]
    pending = []

    def send(group, source, target, mine, every):
        index = used[0]
        used[0] += 1
        for peer, _, device in groups[group]:
            pltpu.make_async_remote_copy(
                src_ref=source(peer),
                dst_ref=target(mine),
                send_sem=sent.at[index],
                recv_sem=wire.at[index],
                device_id=device,
                device_id_type=MESH,
            ).start()
        whole = pltpu.make_async_remote_copy(
            src_ref=every,
            dst_ref=every,
            send_sem=sent.at[index],
            recv_sem=wire.at[index],
            device_id=groups[group][0][2],
            device_id_type=MESH,
        )
        pending.append(whole)

        def wait():
            whole.wait_recv()

        return wait

    def others(ref):
        return ref.at[pl.ds(0, ref.shape[0] - 1)]

    def sends_done():
        while pending:
            pending.pop(0).wait_send()

    loads = [
        pltpu.make_async_copy(momentum_in.at[0], mem["momentum"], local.at[0]),
        pltpu.make_async_copy(gradient_in.at[0], gradient, local.at[1]),
        pltpu.make_async_copy(basis_in, mem["basis"], local.at[2]),
    ]
    for load in loads:
        load.start()
    barrier = pltpu.get_barrier_semaphore()
    partners = 0
    for group in ("z", "xy", "c"):
        for _, _, device in groups[group]:
            pl.semaphore_signal(barrier, inc=1, device_id=device, device_id_type=MESH)
            partners += 1
    for load in loads:
        load.wait()

    for k in range(reps):
        lanes = slice(k * sub, (k + 1) * sub)
        mem["piece"][k] = mem["momentum"][:, lanes] + gradient[:, lanes].astype(jnp.float32)

    def added(ref):
        total = ref[0]
        for s in range(1, ref.shape[0]):
            total = total + ref[s]
        return total

    def scatter_left(it, partial):
        out, got = mem["left_part"].at[it], mem["left_got"].at[it]
        out[...] = partial.reshape(plane, part, rank)
        wait = send("xy", lambda p: out.at[p], lambda s: got.at[s], here, others(got))
        got[here] = out[here]
        return wait

    def gather_left(it):
        full = mem["left"].at[it]
        full[here] = added(mem["left_got"].at[it])
        return send("xy", lambda p: full.at[here], lambda s: full.at[s], here, others(full))

    def left_of(it):
        return mem["left"][it].reshape(m, rank)

    def reduce_right(it):
        now = mem["now"]
        split, other = mem["right_split"].at[it], mem["right_core"].at[it]
        sibling = CORES - 1 - core

        def lanes_of(h):
            return pl.ds(pl.multiple_of(h * half, half), half)

        mean_t = mem["mean_t"][...]
        split[0] = rows_by_rows(mean_t, now[:, lanes_of(sibling)])
        wait_c = send("c", lambda p: split.at[0], lambda s: other, 0, other)
        split[1] = rows_by_rows(mean_t, now[:, lanes_of(core)])
        wait_c()
        out, got = mem["right_z"].at[it], mem["right_got"].at[it]
        out[...] = (split[1] + other[...]).reshape(depth, part_z, half)
        wait_c = send("z", lambda p: out.at[p], lambda s: got.at[s], z, others(got))
        got[z] = out[z]
        mem["gram_part"][it] = transposed_by(now[...], now[...])
        mine = pl.ds(pl.multiple_of(here * part_g, TILE), part_g)
        g_out, g_other = mem["gram_split"].at[it], mem["gram_core"].at[it]
        g_out[...] = mem["gram_part"][it, mine, lanes_of(sibling)]
        wait_g = send("c", lambda p: g_out, lambda s: g_other, 0, g_other)
        wait_g()
        g_all = mem["gram_z"].at[it]
        g_all[z] = mem["gram_part"][it, mine, lanes_of(core)] + g_other[...]
        wait_g = send("z", lambda p: g_all.at[z], lambda s: g_all.at[s], z, others(g_all))
        yield
        wait_c()
        full = mem["right"].at[it]
        full[core, z] = added(got)
        wait_c = send(
            "z", lambda p: full.at[core, z], lambda s: full.at[core, s], z, others(full.at[core])
        )
        wait_g()
        gram = mem["gram"].at[it]
        gram[core, here] = added(g_all)
        wait_g = send(
            "xy",
            lambda p: gram.at[core, here],
            lambda s: gram.at[core, s],
            here,
            others(gram.at[core]),
        )
        yield
        wait_c()
        if it == 0:
            wait_c = send("c", lambda p: full.at[core], lambda s: full.at[s], core, full.at[0])
        else:
            rights = mem["rights"].at[core]
            rights[x] = full[core]
            wait_c = send("x", lambda p: full.at[core], lambda s: rights.at[s], x, others(rights))
        wait_g()
        wait_g = send("c", lambda p: gram.at[core], lambda s: gram.at[s], core, gram.at[0])
        yield wait_c
        wait_g()

    def joined(ref, rows):
        return jnp.concatenate([ref[h].reshape(rows, half) for h in range(CORES)], axis=1)

    def squares_of(factor):
        squares = jnp.sum(factor * factor, axis=0, keepdims=True)
        return jnp.broadcast_to(squares, (TILE, rank))

    def share(group, name, mine, value):
        ref = mem[name]
        ref[mine] = value
        return send(group, lambda p: ref.at[mine], lambda s: ref.at[s], mine, others(ref))

    def rms_of(total):
        return jnp.sqrt(total / jnp.float32(order) + 1e-06)

    chol = Cholesky(mem["chol"])
    middle = chol.groups // 2

    product = None
    for k in range(reps):
        term = rows_by_rows(mem["piece"][k], mem["basis"][k * sub : (k + 1) * sub, :])
        product = term if product is None else product + term
    pl.semaphore_wait(barrier, partners)
    wait_left = scatter_left(0, product * (1.0 / reps))
    exchange = send(
        "x", lambda p: mem["piece"].at[p], lambda s: mem["pieces"].at[s], x, others(mem["pieces"])
    )
    mem["pieces"][x] = mem["piece"][x]
    wait_left()
    wait_left = gather_left(0)
    exchange()
    mem["mean"][...] = added(mem["pieces"]) * (1.0 / reps)
    mem["mean_t"][...] = jnp.transpose(mem["mean"][...])
    wait_left()

    mem["now"][...] = left_of(0)
    stages = reduce_right(0)
    next(stages)
    next(stages)
    next(stages)()
    right = joined(mem["right"].at[0], sub)
    wait_left = scatter_left(1, rows_by_rows(mem["mean"][...], right))
    for _ in stages:
        pass
    chol.load(joined(mem["gram"].at[0], rank))
    chol.run(0, middle)
    wait_left()
    wait_left = gather_left(1)
    chol.run(middle, chol.groups)
    inverse = chol.inverse()
    wait_left()
    left = by_transposed(left_of(1), inverse)
    mem["now"][...] = left

    stages = reduce_right(1)
    next(stages)
    squares = squares_of(by_transposed(joined(mem["right"].at[0], sub), inverse))
    wait_squares = share("x", "square_x", x, squares)
    next(stages)
    wait_squares()
    wait_squares = share("y", "square_y", y, added(mem["square_x"]))
    sends_done()
    wait_right = next(stages)
    wait_squares()
    scale = (1.0 / rms_of(added(mem["square_y"])))[:1, :]
    mem["scale"][...] = jnp.broadcast_to(scale, (TILE, rank))
    across = jnp.transpose(jnp.broadcast_to(scale, (LANES, rank)))[:, :1]
    for _ in stages:
        pass
    chol.load(joined(mem["gram"].at[1], rank) * scale * across)
    chol.run(0, middle)
    wait_right()
    rights = mem["rights"]
    wait_right = send(
        "c", lambda p: rights.at[core], lambda s: rights.at[s], core, rights.at[0]
    )
    chol.run(middle, chol.groups)
    inverse = chol.inverse()
    scale = mem["scale"][:1, :]
    wait_right()
    squares = None
    for k in range(reps):
        gathered = [rights[h, k].reshape(sub, half) for h in range(CORES)]
        factor = by_transposed(jnp.concatenate(gathered, axis=1) * scale, inverse)
        factor_out[k * sub : (k + 1) * sub, :] = factor
        term = squares_of(factor)
        squares = term if squares is None else squares + term
    wait_squares = share("y", "square_last", y, squares)
    ortho_out[...] = by_transposed(mem["now"][...] * scale, inverse)
    sends_done()
    wait_squares()
    rms_out[...] = rms_of(added(mem["square_last"]))
    assert used[0] == sent.shape[0]


def in_two(x):
    high = x.astype(jnp.bfloat16)
    return high, (x - high.astype(jnp.float32)).astype(jnp.bfloat16)


def three_products(a, b):
    (ah, al), (bh, bl) = a, b

    def one(p, q):
        return lax.dot_general(
            p, q, (((1,), (1,)), ((), ())), preferred_element_type=jnp.float32
        )

    return (one(al, bh) + one(ah, bl)) + one(ah, bh)


def finish_kernel(rate, ortho, rms, factor, momentum, gradient, weight, new_momentum, new_weight, new_basis):
    basis = factor[...] / rms[:1, :]
    new_basis[...] = basis
    left = in_two(ortho[...])
    buffer = momentum[0] + gradient[0].astype(jnp.float32)
    new_momentum[0] = buffer - (1.0 - beta_mom) * three_products(left, in_two(factor[...]))
    new_weight[...] = weight[...] - rate * three_products(left, in_two(basis))


def step(mesh, momentum, gradient, weight, right_basis):
    reps, cols = mesh.shape["rep"], mesh.shape["col"]
    depth = mesh.shape["row"] // CORES
    _, m, n = momentum.shape
    sub, rank = n // reps, right_basis.shape[1]
    order = n * cols
    half, plane = rank // CORES, reps * cols
    part, part_z, part_g = m // plane, sub // depth, rank // plane
    f32 = jnp.float32
    shapes = {
        "momentum": (m, n),
        "basis": (n, rank),
        "piece": (reps, m, sub),
        "pieces": (reps, m, sub),
        "mean": (m, sub),
        "mean_t": (sub, m),
        "left_part": (2, plane, part, rank),
        "left_got": (2, plane, part, rank),
        "left": (2, plane, part, rank),
        "now": (m, rank),
        "gram_part": (2, rank, rank),
        "right_split": (2, CORES, sub, half),
        "right_core": (2, sub, half),
        "gram_split": (2, part_g, half),
        "gram_core": (2, part_g, half),
        "right_z": (2, depth, part_z, half),
        "right_got": (2, depth, part_z, half),
        "right": (2, CORES, depth, part_z, half),
        "gram_z": (2, depth, part_g, half),
        "gram": (2, CORES, plane, part_g, half),
        "square_x": (reps, TILE, rank),
        "square_y": (cols, TILE, rank),
        "square_last": (cols, TILE, rank),
        "scale": (TILE, rank),
        "chol": (rank, 2 * rank),
        "rights": (CORES, reps, depth, part_z, half),
    }
    copies = 25
    hbm = pl.BlockSpec(memory_space=pl.ANY)
    vmem = pl.BlockSpec(memory_space=pltpu.VMEM)
    ortho, factor, rms = pl.pallas_call(
        functools.partial(step_kernel, (reps, cols, depth, m, n, sub, rank, order)),
        out_shape=[
            jax.ShapeDtypeStruct((m, rank), f32),
            jax.ShapeDtypeStruct((n, rank), f32),
            jax.ShapeDtypeStruct((TILE, rank), f32),
        ],
        in_specs=[hbm] * 3,
        out_specs=[vmem] * 3,
        scratch_shapes=[
            {name: pltpu.VMEM(dims, f32) for name, dims in shapes.items()},
            pltpu.VMEM((m, n), gradient.dtype),
            pltpu.SemaphoreType.DMA((3,)),
            pltpu.SemaphoreType.DMA((copies,)),
            pltpu.SemaphoreType.DMA((copies,)),
        ],
        compiler_params=pltpu.CompilerParams(
            collective_id=0, has_side_effects=True, vmem_limit_bytes=58 << 20
        ),
        name="dion_step",
    )(momentum, gradient, right_basis)
    tile = min(256, n)
    whole = pl.BlockSpec((m, rank), lambda i: (0, 0))
    plain = pl.BlockSpec((m, tile), lambda i: (0, i))
    stack = pl.BlockSpec((1, m, tile), lambda i: (0, 0, i))
    lines = pl.BlockSpec((tile, rank), lambda i: (i, 0))
    rate = learn_rate * (order / rank) ** 0.5
    return pl.pallas_call(
        functools.partial(finish_kernel, rate),
        grid=(n // tile,),
        out_shape=[
            jax.ShapeDtypeStruct((1, m, n), f32),
            jax.ShapeDtypeStruct((m, n), f32),
            jax.ShapeDtypeStruct((n, rank), f32),
        ],
        in_specs=[whole, pl.BlockSpec((TILE, rank), lambda i: (0, 0)), lines, stack, stack, plain],
        out_specs=[stack, plain, lines],
        compiler_params=pltpu.CompilerParams(vmem_limit_bytes=58 << 20),
        name="dion_finish",
    )(ortho, rms, factor, momentum, gradient, weight)


def solution(mesh):
    return jax.shard_map(
        functools.partial(step, mesh),
        mesh=mesh,
        in_specs=(P("rep", "row", "col"), P("rep", "row", "col"), P("row", "col"), P("col", None)),
        out_specs=(P("rep", "row", "col"), P("row", "col"), P("col", None)),
        check_vma=False,
    )
```

```python
import functools

import jax
import jax.numpy as jnp
from jax import lax
from jax.experimental import pallas as pl
from jax.experimental.pallas import tpu as pltpu
from jax.sharding import PartitionSpec as P

beta_mom = 0.95
learn_rate = 0.05
CORES = 2
TILE = 8
LANES = 128
HIGHEST = lax.Precision.HIGHEST
MESH = pl.DeviceIdType.MESH


def dot(a, b, over):
    return lax.dot_general(
        a, b, (over, ((), ())), precision=HIGHEST, preferred_element_type=jnp.float32
    )


def rows_by_rows(a, b):
    return dot(a, b, ((1,), (0,)))


def by_transposed(a, b):
    return dot(a, b, ((1,), (1,)))


def transposed_by(a, b):
    return dot(a, b, ((0,), (0,)))


def in_three(x):
    high = x.astype(jnp.bfloat16).astype(jnp.float32)
    rest = x - high
    middle = rest.astype(jnp.bfloat16).astype(jnp.float32)
    return high, middle, rest - middle


def thin_product(a, b):
    (ah, am, al), (bh, bm, bl) = in_three(a), in_three(b)
    left = jnp.concatenate([ah, ah, am, am, ah, al], axis=0).astype(jnp.bfloat16)
    right = jnp.concatenate([bh, bm, bh, bm, bl, bh], axis=0).astype(jnp.bfloat16)
    return lax.dot_general(
        left, right, (((0,), (0,)), ((), ())), preferred_element_type=jnp.float32
    )


class Cholesky:
    group = 4

    def __init__(self, work):
        self.work = work
        self.n = work.shape[0]
        self.panel = min(128, self.n)
        self.groups = self.n // (TILE * self.group)

    def load(self, gram):
        n = self.n
        self.work[:, :n] = gram
        eye = lax.broadcasted_iota(jnp.int32, (n, n), 0) == lax.broadcasted_iota(
            jnp.int32, (n, n), 1
        )
        self.work[:, n:] = jnp.where(eye, 1.0, 0.0)

    def run(self, first, last):
        work, n, size, count = self.work, self.n, self.panel, self.group
        step = TILE * count
        base = (first * step // size) * size
        wide = (TILE, LANES)
        tiles = 2 * n // LANES
        sub = lax.broadcasted_iota(jnp.int32, wide, 0)
        in_panel = lax.broadcasted_iota(jnp.int32, (size, 1), 0)

        def spread(block, lane):
            return jnp.broadcast_to(block[:, lane : lane + 1], wide)

        def body(t, carry):
            start = pl.multiple_of(t * step, step)
            rows, small = [], []
            for b in range(count):
                got = work[pl.ds(start + TILE * b, TILE), :]
                rows.append([got[:, k * LANES : (k + 1) * LANES] for k in range(tiles)])
                small.append(pltpu.roll(got[:, :n], lax.rem(n - start, n), 1)[:, :LANES])
            for b in range(count):
                columns = [spread(small[b], TILE * b + i) for i in range(TILE)]
                below = {
                    c: [spread(small[c], TILE * b + i) for i in range(TILE)]
                    for c in range(b + 1, count)
                }
                a = {
                    (r, i): jnp.broadcast_to(columns[i][r : r + 1, :], wide)
                    for i in range(TILE)
                    for r in range(i, TILE)
                }
                low, inv = {}, {}
                for i in range(TILE):
                    root = lax.rsqrt(a[i, i])
                    inv[i, i] = root
                    for r in range(i + 1, TILE):
                        low[r, i] = a[r, i] * root
                    for r in range(i + 1, TILE):
                        for c in range(i + 1, r + 1):
                            a[r, c] = a[r, c] - low[r, i] * low[c, i]
                    for c in range(i):
                        acc = low[i, c] * inv[c, c]
                        for k in range(c + 1, i):
                            acc = acc + low[i, k] * inv[k, c]
                        inv[i, c] = -(acc * root)
                sums = [None] * (tiles + 1)
                source = rows[b] + [small[b]]
                for c in range(TILE):
                    column = jnp.where(sub == c, inv[c, c], 0.0)
                    for r in range(c + 1, TILE):
                        column = jnp.where(sub == r, inv[r, c], column)
                    for k in range(tiles + 1):
                        term = column * source[k][c : c + 1, :]
                        sums[k] = term if sums[k] is None else sums[k] + term
                rows[b], small[b] = sums[:tiles], sums[tiles]
                for c in range(b + 1, count):
                    for i in range(TILE):
                        lower = below[c][0] * inv[i, 0]
                        for k in range(1, i + 1):
                            lower = lower + below[c][k] * inv[i, k]
                        rows[c] = [rows[c][k] - lower * rows[b][k][i : i + 1, :] for k in range(tiles)]
                        small[c] = small[c] - lower * small[b][i : i + 1, :]
            done = jnp.concatenate([jnp.concatenate(r, axis=1) for r in rows], axis=0)
            work[pl.ds(start, step), :] = done
            update = thin_product(done[:, base : base + size], done)
            keep = in_panel > start + (step - 1) - base
            work[base : base + size, :] = work[base : base + size, :] - jnp.where(keep, update, 0.0)
            return carry

        lax.fori_loop(first, last, body, 0)
        end = base + size
        if last * step == end and end < n:
            done = work[base:end, :]
            work[end:, :] = work[end:, :] - transposed_by(done[:, end:n], done)

    def inverse(self):
        return self.work[:, self.n :]


def step_kernel(shape, momentum_in, gradient_in, basis_in, ortho_out, factor_out, rms_out, mem, gradient, local, sent, wire):
    reps, cols, depth, m, n, sub, rank, order = shape
    row = lax.axis_index("row")
    core = lax.rem(row, CORES)
    z, y, x = lax.div(row, CORES), lax.axis_index("col"), lax.axis_index("rep")
    plane = reps * cols
    here = x * cols + y
    half = rank // CORES
    part, part_z, part_g = m // plane, sub // depth, rank // plane

    def far_first(size):
        return sorted(range(1, size), key=lambda i: -min(i, size - i))

    def line(size, me, device):
        return [
            (lax.rem(me + i, size), lax.rem(me + size - i, size), device(lax.rem(me + i, size)))
            for i in far_first(size)
        ]

    def sheet():
        pairs = [(i, j) for i in range(reps) for j in range(cols) if i or j]
        pairs.sort(key=lambda p: -(min(p[0], reps - p[0]) + min(p[1], cols - p[1])))
        out = []
        for i, j in pairs:
            px, py = lax.rem(x + i, reps), lax.rem(y + j, cols)
            ox, oy = lax.rem(x + reps - i, reps), lax.rem(y + cols - j, cols)
            out.append((px * cols + py, ox * cols + oy, {"rep": px, "col": py}))
        return out

    groups = {
        "x": line(reps, x, lambda p: {"rep": p}),
        "y": line(cols, y, lambda p: {"col": p}),
        "z": line(depth, z, lambda p: {"row": p * CORES + core}),
        "c": line(CORES, core, lambda p: {"row": z * CORES + p}),
        "xy": sheet(),
    }
    used = [0]
    pending = []

    def send(group, source, target, mine, every):
        index = used[0]
        used[0] += 1
        for peer, _, device in groups[group]:
            pltpu.make_async_remote_copy(
                src_ref=source(peer),
                dst_ref=target(mine),
                send_sem=sent.at[index],
                recv_sem=wire.at[index],
                device_id=device,
                device_id_type=MESH,
            ).start()
        whole = pltpu.make_async_remote_copy(
            src_ref=every,
            dst_ref=every,
            send_sem=sent.at[index],
            recv_sem=wire.at[index],
            device_id=groups[group][0][2],
            device_id_type=MESH,
        )
        pending.append(whole)

        def wait():
            whole.wait_recv()

        return wait

    def others(ref):
        return ref.at[pl.ds(0, ref.shape[0] - 1)]

    def sends_done():
        while pending:
            pending.pop(0).wait_send()

    loads = [
        pltpu.make_async_copy(momentum_in.at[0], mem["momentum"], local.at[0]),
        pltpu.make_async_copy(gradient_in.at[0], gradient, local.at[1]),
        pltpu.make_async_copy(basis_in, mem["basis"], local.at[2]),
    ]
    for load in loads:
        load.start()
    barrier = pltpu.get_barrier_semaphore()
    partners = 0
    for group in ("z", "xy", "c"):
        for _, _, device in groups[group]:
            pl.semaphore_signal(barrier, inc=1, device_id=device, device_id_type=MESH)
            partners += 1
    for load in loads:
        load.wait()

    for k in range(reps):
        lanes = slice(k * sub, (k + 1) * sub)
        mem["piece"][k] = mem["momentum"][:, lanes] + gradient[:, lanes].astype(jnp.float32)

    def added(ref):
        total = ref[0]
        for s in range(1, ref.shape[0]):
            total = total + ref[s]
        return total

    def scatter_left(it, partial):
        out, got = mem["left_part"].at[it], mem["left_got"].at[it]
        out[...] = partial.reshape(plane, part, rank)
        wait = send("xy", lambda p: out.at[p], lambda s: got.at[s], here, others(got))
        got[here] = out[here]
        return wait

    def gather_left(it):
        full = mem["left"].at[it]
        full[here] = added(mem["left_got"].at[it])
        return send("xy", lambda p: full.at[here], lambda s: full.at[s], here, others(full))

    def left_of(it):
        return mem["left"][it].reshape(m, rank)

    def reduce_right(it):
        now = mem["now"]
        split, other = mem["right_split"].at[it], mem["right_core"].at[it]
        sibling = CORES - 1 - core

        def lanes_of(h):
            return pl.ds(pl.multiple_of(h * half, half), half)

        mean_t = mem["mean_t"][...]
        split[0] = rows_by_rows(mean_t, now[:, lanes_of(sibling)])
        wait_c = send("c", lambda p: split.at[0], lambda s: other, 0, other)
        split[1] = rows_by_rows(mean_t, now[:, lanes_of(core)])
        wait_c()
        out, got = mem["right_z"].at[it], mem["right_got"].at[it]
        out[...] = (split[1] + other[...]).reshape(depth, part_z, half)
        wait_c = send("z", lambda p: out.at[p], lambda s: got.at[s], z, others(got))
        got[z] = out[z]
        mem["gram_part"][it] = transposed_by(now[...], now[...])
        mine = pl.ds(pl.multiple_of(here * part_g, TILE), part_g)
        g_out, g_other = mem["gram_split"].at[it], mem["gram_core"].at[it]
        g_out[...] = mem["gram_part"][it, mine, lanes_of(sibling)]
        wait_g = send("c", lambda p: g_out, lambda s: g_other, 0, g_other)
        wait_g()
        g_all = mem["gram_z"].at[it]
        g_all[z] = mem["gram_part"][it, mine, lanes_of(core)] + g_other[...]
        wait_g = send("z", lambda p: g_all.at[z], lambda s: g_all.at[s], z, others(g_all))
        yield
        wait_c()
        full = mem["right"].at[it]
        full[core, z] = added(got)
        wait_c = send(
            "z", lambda p: full.at[core, z], lambda s: full.at[core, s], z, others(full.at[core])
        )
        wait_g()
        gram = mem["gram"].at[it]
        gram[core, here] = added(g_all)
        wait_g = send(
            "xy",
            lambda p: gram.at[core, here],
            lambda s: gram.at[core, s],
            here,
            others(gram.at[core]),
        )
        yield
        wait_c()
        wait_c = send("c", lambda p: full.at[core], lambda s: full.at[s], core, full.at[0])
        wait_g()
        wait_g = send("c", lambda p: gram.at[core], lambda s: gram.at[s], core, gram.at[0])
        yield wait_c
        wait_g()

    def reduce_right_gram_first():
        it, now = 1, mem["now"]
        split, other = mem["right_split"].at[it], mem["right_core"].at[it]
        sibling = CORES - 1 - core

        def lanes_of(h):
            return pl.ds(pl.multiple_of(h * half, half), half)

        mem["gram_part"][it] = transposed_by(now[...], now[...])
        mine = pl.ds(pl.multiple_of(here * part_g, TILE), part_g)
        g_out, g_other = mem["gram_split"].at[it], mem["gram_core"].at[it]
        g_out[...] = mem["gram_part"][it, mine, lanes_of(sibling)]
        wait_g = send("c", lambda p: g_out, lambda s: g_other, 0, g_other)
        mean_t = mem["mean_t"][...]
        split[0] = rows_by_rows(mean_t, now[:, lanes_of(sibling)])
        wait_c = send("c", lambda p: split.at[0], lambda s: other, 0, other)
        wait_g()
        g_all = mem["gram_z"].at[it]
        g_all[z] = mem["gram_part"][it, mine, lanes_of(core)] + g_other[...]
        wait_g = send("z", lambda p: g_all.at[z], lambda s: g_all.at[s], z, others(g_all))
        split[1] = rows_by_rows(mean_t, now[:, lanes_of(core)])
        wait_c()
        out, got = mem["right_z"].at[it], mem["right_got"].at[it]
        out[...] = (split[1] + other[...]).reshape(depth, part_z, half)
        wait_c = send("z", lambda p: out.at[p], lambda s: got.at[s], z, others(got))
        got[z] = out[z]
        yield
        wait_g()
        gram = mem["gram"].at[it]
        gram[core, here] = added(g_all)
        wait_g = send(
            "xy",
            lambda p: gram.at[core, here],
            lambda s: gram.at[core, s],
            here,
            others(gram.at[core]),
        )
        wait_c()
        full = mem["right"].at[it]
        full[core, z] = added(got)
        wait_c = send(
            "z", lambda p: full.at[core, z], lambda s: full.at[core, s], z, others(full.at[core])
        )
        yield
        wait_g()
        wait_g = send("c", lambda p: gram.at[core], lambda s: gram.at[s], core, gram.at[0])
        wait_g()
        yield
        wait_c()
        rights = mem["rights"]
        by_x = rights.at[core]
        by_x[x] = full[core]
        wait_c = send("x", lambda p: full.at[core], lambda s: by_x.at[s], x, others(by_x))
        yield
        wait_c()
        wait_c = send("c", lambda p: rights.at[core], lambda s: rights.at[s], core, rights.at[0])
        yield
        wait_c()

    def joined(ref, rows):
        return jnp.concatenate([ref[h].reshape(rows, half) for h in range(CORES)], axis=1)

    def squares_of(factor):
        squares = jnp.sum(factor * factor, axis=0, keepdims=True)
        return jnp.broadcast_to(squares, (TILE, rank))

    def share(group, name, mine, value):
        ref = mem[name]
        ref[mine] = value
        return send(group, lambda p: ref.at[mine], lambda s: ref.at[s], mine, others(ref))

    def rms_of(total):
        return jnp.sqrt(total / jnp.float32(order) + 1e-06)

    chol = Cholesky(mem["chol"])
    middle = chol.groups // 2

    product = None
    for k in range(reps):
        term = rows_by_rows(mem["piece"][k], mem["basis"][k * sub : (k + 1) * sub, :])
        product = term if product is None else product + term
    pl.semaphore_wait(barrier, partners)
    wait_left = scatter_left(0, product * (1.0 / reps))
    exchange = send(
        "x", lambda p: mem["piece"].at[p], lambda s: mem["pieces"].at[s], x, others(mem["pieces"])
    )
    mem["pieces"][x] = mem["piece"][x]
    wait_left()
    wait_left = gather_left(0)
    exchange()
    mem["mean"][...] = added(mem["pieces"]) * (1.0 / reps)
    mem["mean_t"][...] = jnp.transpose(mem["mean"][...])
    wait_left()

    mem["now"][...] = left_of(0)
    stages = reduce_right(0)
    next(stages)
    next(stages)
    next(stages)()
    right = joined(mem["right"].at[0], sub)
    wait_left = scatter_left(1, rows_by_rows(mem["mean"][...], right))
    for _ in stages:
        pass
    chol.load(joined(mem["gram"].at[0], rank))
    chol.run(0, middle)
    wait_left()
    wait_left = gather_left(1)
    chol.run(middle, chol.groups)
    inverse = chol.inverse()
    wait_left()
    left = by_transposed(left_of(1), inverse)
    mem["now"][...] = left

    stages = reduce_right_gram_first()
    next(stages)
    squares = squares_of(by_transposed(joined(mem["right"].at[0], sub), inverse))
    wait_squares = share("x", "square_x", x, squares)
    next(stages)
    wait_squares()
    wait_squares = share("y", "square_y", y, added(mem["square_x"]))
    sends_done()
    wait_squares()
    scale = (1.0 / rms_of(added(mem["square_y"])))[:1, :]
    mem["scale"][...] = jnp.broadcast_to(scale, (TILE, rank))
    across = jnp.transpose(jnp.broadcast_to(scale, (LANES, rank)))[:, :1]
    next(stages)
    chol.load(joined(mem["gram"].at[1], rank) * scale * across)
    rights = mem["rights"]
    chol.run(0, 1)
    next(stages)
    chol.run(1, middle)
    chol.run(middle, chol.groups - 2)
    next(stages)
    chol.run(chol.groups - 2, chol.groups)
    inverse = chol.inverse()
    scale = mem["scale"][:1, :]
    for _ in stages:
        pass
    squares = None
    for k in range(reps):
        gathered = [rights[h, k].reshape(sub, half) for h in range(CORES)]
        factor = by_transposed(jnp.concatenate(gathered, axis=1) * scale, inverse)
        factor_out[k * sub : (k + 1) * sub, :] = factor
        term = squares_of(factor)
        squares = term if squares is None else squares + term
    wait_squares = share("y", "square_last", y, squares)
    ortho_out[...] = by_transposed(mem["now"][...] * scale, inverse)
    sends_done()
    wait_squares()
    rms_out[...] = rms_of(added(mem["square_last"]))
    assert used[0] == sent.shape[0]


def in_two(x):
    high = x.astype(jnp.bfloat16)
    return high, (x - high.astype(jnp.float32)).astype(jnp.bfloat16)


def three_products(a, b):
    (ah, al), (bh, bl) = a, b

    def one(p, q):
        return lax.dot_general(
            p, q, (((1,), (1,)), ((), ())), preferred_element_type=jnp.float32
        )

    return (one(al, bh) + one(ah, bl)) + one(ah, bh)


def finish_kernel(rate, ortho, rms, factor, momentum, gradient, weight, new_momentum, new_weight, new_basis):
    basis = factor[...] / rms[:1, :]
    new_basis[...] = basis
    left = in_two(ortho[...])
    buffer = momentum[0] + gradient[0].astype(jnp.float32)
    new_momentum[0] = buffer - (1.0 - beta_mom) * three_products(left, in_two(factor[...]))
    new_weight[...] = weight[...] - rate * three_products(left, in_two(basis))


def step(mesh, momentum, gradient, weight, right_basis):
    reps, cols = mesh.shape["rep"], mesh.shape["col"]
    depth = mesh.shape["row"] // CORES
    _, m, n = momentum.shape
    sub, rank = n // reps, right_basis.shape[1]
    order = n * cols
    half, plane = rank // CORES, reps * cols
    part, part_z, part_g = m // plane, sub // depth, rank // plane
    f32 = jnp.float32
    shapes = {
        "momentum": (m, n),
        "basis": (n, rank),
        "piece": (reps, m, sub),
        "pieces": (reps, m, sub),
        "mean": (m, sub),
        "mean_t": (sub, m),
        "left_part": (2, plane, part, rank),
        "left_got": (2, plane, part, rank),
        "left": (2, plane, part, rank),
        "now": (m, rank),
        "gram_part": (2, rank, rank),
        "right_split": (2, CORES, sub, half),
        "right_core": (2, sub, half),
        "gram_split": (2, part_g, half),
        "gram_core": (2, part_g, half),
        "right_z": (2, depth, part_z, half),
        "right_got": (2, depth, part_z, half),
        "right": (2, CORES, depth, part_z, half),
        "gram_z": (2, depth, part_g, half),
        "gram": (2, CORES, plane, part_g, half),
        "square_x": (reps, TILE, rank),
        "square_y": (cols, TILE, rank),
        "square_last": (cols, TILE, rank),
        "scale": (TILE, rank),
        "chol": (rank, 2 * rank),
        "rights": (CORES, reps, depth, part_z, half),
    }
    copies = 25
    hbm = pl.BlockSpec(memory_space=pl.ANY)
    vmem = pl.BlockSpec(memory_space=pltpu.VMEM)
    ortho, factor, rms = pl.pallas_call(
        functools.partial(step_kernel, (reps, cols, depth, m, n, sub, rank, order)),
        out_shape=[
            jax.ShapeDtypeStruct((m, rank), f32),
            jax.ShapeDtypeStruct((n, rank), f32),
            jax.ShapeDtypeStruct((TILE, rank), f32),
        ],
        in_specs=[hbm] * 3,
        out_specs=[vmem] * 3,
        scratch_shapes=[
            {name: pltpu.VMEM(dims, f32) for name, dims in shapes.items()},
            pltpu.VMEM((m, n), gradient.dtype),
            pltpu.SemaphoreType.DMA((3,)),
            pltpu.SemaphoreType.DMA((copies,)),
            pltpu.SemaphoreType.DMA((copies,)),
        ],
        compiler_params=pltpu.CompilerParams(
            collective_id=0, has_side_effects=True, vmem_limit_bytes=58 << 20
        ),
        name="dion_step",
    )(momentum, gradient, right_basis)
    tile = min(256, n)
    whole = pl.BlockSpec((m, rank), lambda i: (0, 0))
    plain = pl.BlockSpec((m, tile), lambda i: (0, i))
    stack = pl.BlockSpec((1, m, tile), lambda i: (0, 0, i))
    lines = pl.BlockSpec((tile, rank), lambda i: (i, 0))
    rate = learn_rate * (order / rank) ** 0.5
    return pl.pallas_call(
        functools.partial(finish_kernel, rate),
        grid=(n // tile,),
        out_shape=[
            jax.ShapeDtypeStruct((1, m, n), f32),
            jax.ShapeDtypeStruct((m, n), f32),
            jax.ShapeDtypeStruct((n, rank), f32),
        ],
        in_specs=[whole, pl.BlockSpec((TILE, rank), lambda i: (0, 0)), lines, stack, stack, plain],
        out_specs=[stack, plain, lines],
        compiler_params=pltpu.CompilerParams(vmem_limit_bytes=58 << 20),
        name="dion_finish",
    )(ortho, rms, factor, momentum, gradient, weight)


def solution(mesh):
    return jax.shard_map(
        functools.partial(step, mesh),
        mesh=mesh,
        in_specs=(P("rep", "row", "col"), P("rep", "row", "col"), P("row", "col"), P("col", None)),
        out_specs=(P("rep", "row", "col"), P("row", "col"), P("col", None)),
        check_vma=False,
    )
```
